32 devices in a mesh: row: 4 (over y, core), col: 8 (over z, x).
Axes of the slice: x: 2, y: 2, z: 4, core: 2. Of those that a mesh axis runs over, the one named last changes fastest.
Arguments:
- amplitudes: float32 [256, 2, 16384], P('row', None, 'col'), may hold values from -6 to 6
- integrals: bfloat16 [2, 16384, 16384], P(None, 'col', 'row'), may hold values from -0.046875 to 0.046875
- screen: int32 [2, 128, 128], P(None, 'col', 'row'), may hold values 0 or 1
- mirror: int32 [16384], replicated, may hold values from 0 to 16383, as said below
- denominators: float32 [256, 2, 16384], P('col', None, 'row'), may hold values from 0.5 to 4
Outputs:
- update: float32 [256, 2, 16384], P('col', None, 'row')
The draws below stay inside these ranges and needn't reach their ends.
Inputs may be any that keep to these rules, and one draw needn't show every extreme that they name: mirror is a permutation; mirror[p] lies in the tile of 128 positions numbered (p // 128 + 16384 // 256) modulo 16384 // 128.
All inputs are finite; a program needn't handle non-finite values. No bound on the sum of `screen` on one device may be relied on, other than what follows from the above.
Results may differ from the reference program's by a relative error of at most 0.0029.
Values may be sent and summed in bfloat16 or wider, within the bound.
A program may use at most 192 MiB of HBM per device.

```python
import math
import jax
import jax.numpy as jnp
from jax import lax

OCC_PAIRS = 256
PAIRS = 16384
TILE = 128


def draw_mirror(key, part):
    tile_count = PAIRS // TILE
    tile_keys = jax.random.split(jax.random.fold_in(key, 7), tile_count)
    within = jax.vmap(lambda k: jax.random.permutation(k, TILE))(tile_keys).astype(jnp.int32)
    target = (jnp.arange(tile_count, dtype=jnp.int32) + tile_count // 2) % tile_count
    return (target[:, None] * TILE + within).reshape(PAIRS).astype(jnp.int32)


def plant(drawn, key, least, top_value):
    extent = drawn.shape
    spot = [jax.random.randint(jax.random.fold_in(key, axis), (), 0, extent[axis]) for axis in range(len(extent))]
    drawn = drawn.at[tuple(spot)].set(least)
    longest = extent.index(max(extent))
    spot[longest] = (spot[longest] + 1) % extent[longest]
    return drawn.at[tuple(spot)].set(top_value)


def block_levels(rng, shape, cuts, least, top_value):
    def one(dim, shards_of):
        steps = jax.random.uniform(jax.random.fold_in(jax.random.fold_in(rng, 6), dim), (shards_of,), jnp.float32, least / len(cuts), top_value / len(cuts))
        return jnp.repeat(jnp.exp(steps), shape[dim] // shards_of).reshape((-1,) + (1,) * (len(shape) - dim - 1))

    level = one(*cuts[0])
    for cut in cuts[1:]:
        level = level * one(*cut)
    return level


def gaussian(rng, extent, scale, reach, cuts=(), kind=jnp.bfloat16):
    result = scale * jax.random.normal(rng, extent, jnp.float32)
    if cuts:
        result = result * block_levels(rng, extent, cuts, -0.22, 0.18)
    return jnp.clip(result, -reach, reach).astype(kind)


def setup_inputs(seed: int = 0) -> dict:
    keys = jax.random.split(jax.random.key(seed), 6)
    amplitudes = gaussian(keys[0], (OCC_PAIRS, 2, PAIRS), 1.0, 6.0, ((0, 4), (2, 8)), jnp.float32)
    integrals = gaussian(keys[1], (2, PAIRS, PAIRS), PAIRS ** -0.5, 0.046875, ((1, 8), (2, 4)))
    screen = plant((jax.random.randint(keys[2], (2, PAIRS // TILE, PAIRS // TILE), 0, 3) < 2).astype(jnp.int32), jax.random.fold_in(keys[2], 1), 0, 1)
    mirror = draw_mirror(jax.random.fold_in(keys[5], 71), 0)
    denominators = jnp.clip(jnp.exp(math.log(4.0) - 2.0794415 * jax.random.uniform(keys[4], (OCC_PAIRS, 2, PAIRS), jnp.float32) ** block_levels(keys[4], (OCC_PAIRS, 2, PAIRS), ((0, 8), (2, 4)), -0.2, 0.2)), 0.5, 4.0)
    return dict(amplitudes=amplitudes, integrals=integrals, screen=screen, mirror=mirror, denominators=denominators)


def one_sign(signed_part, block, kept_tiles):
    tile_count = PAIRS // TILE

    def step(total, tile):
        start = (tile * TILE).astype(jnp.int32)
        rows = lax.dynamic_slice_in_dim(block, start, TILE, 0)
        keep = jnp.repeat(lax.dynamic_slice_in_dim(kept_tiles, tile, 1, 0)[0].astype(rows.dtype), TILE)
        columns = lax.dynamic_slice_in_dim(signed_part, start, TILE, 1)
        product = jnp.dot(columns, rows * keep[None, :], preferred_element_type=jnp.float32)
        return total + product, None

    total, _ = lax.scan(step, jnp.zeros((OCC_PAIRS, PAIRS), jnp.float32), jnp.arange(tile_count, dtype=jnp.int32))
    return total


def reference(amplitudes, integrals, screen, mirror, denominators):
    direct = amplitudes[:, 0, :]
    flipped = jnp.take(amplitudes[:, 1, :], mirror, axis=1)
    plus_amp = (direct + flipped).astype(jnp.bfloat16)
    minus_amp = (direct - flipped).astype(jnp.bfloat16)
    plus_sum = one_sign(plus_amp, integrals[0], screen[0])
    minus_sum = one_sign(minus_amp, integrals[1], screen[1])
    first = 0.5 * (plus_sum + minus_sum)
    second = jnp.zeros_like(first).at[:, mirror].set(0.5 * (plus_sum - minus_sum))
    return jnp.stack([first, second], axis=1) / denominators
```

```python
import functools

import jax
import jax.numpy as jnp
from jax import lax
from jax.experimental import pallas as pl
from jax.experimental.pallas import tpu as pltpu
from jax.sharding import PartitionSpec as P

TILE = 128
F32, BF16 = jnp.float32, jnp.bfloat16


def flip(x, bits):
    result = x
    place = 0
    while bits >> place:
        if bits >> place & 1:
            result = result + (1 - 2 * (x // (1 << place) % 2)) * (1 << place)
        place += 1
    return result


def position(owner, me, bits):
    total = 0
    for i in range(bits):
        differs = (owner // (1 << i) + me // (1 << i)) % 2
        total = total + differs * (1 << (bits - 1 - i))
    return total


def kernel(sizes, direct, mirrored, cd_lane, ab_lane, mask, integrals, out0, out1,
           held, arrived, signed, acc, *rest):
    rows, cols, groups, chunk = sizes
    row_bits, col_bits = rows.bit_length() - 1, cols.bit_length() - 1
    sends, recvs = rest[:col_bits], rest[col_bits:2 * col_bits]
    msend, mrecv, k_sem, f_sem, g_sem, r_sem, m_sem = rest[2 * col_bits:]
    occ, cd_width = direct.shape
    ab_width = out0.shape[1]
    own = out0.shape[0]
    part = own // groups
    per_row = occ // own
    chunks = ab_width // chunk
    pieces = groups * chunks
    row_me, col_me = lax.axis_index("row"), lax.axis_index("col")

    barrier = pltpu.get_barrier_semaphore()
    for b in range(col_bits):
        pl.semaphore_signal(barrier, inc=1, device_id={"col": flip(col_me, 1 << b)}, device_id_type=pl.DeviceIdType.MESH)
    for b in range(row_bits):
        pl.semaphore_signal(barrier, inc=1, device_id={"row": flip(row_me, 1 << b)}, device_id_type=pl.DeviceIdType.MESH)
    pl.semaphore_wait(barrier, col_bits + row_bits)

    def remote(src, dst, sem, target):
        return pltpu.make_async_remote_copy(
            src_ref=src, dst_ref=dst, send_sem=sem[0], recv_sem=sem[1],
            device_id=target, device_id_type=pl.DeviceIdType.MESH)

    def f_copy(g, k):
        at = pl.ds(k * own + g * part, part)
        i = g * per_row + k
        return remote(mirrored.at[at, :], arrived.at[at, :], (f_sem.at[0, i], f_sem.at[1, i]),
                      {"col": flip(col_me, cols // 2)})

    def k_copy(j):
        c, s = j // 2, j % 2
        return pltpu.make_async_copy(
            integrals.at[s, :, pl.ds(pl.multiple_of(c * chunk, chunk), chunk)], held.at[j], k_sem.at[j])

    def gather_copies(g, stage, k):
        bit = row_bits - 1 - stage
        copies = []
        for t in range(1 << stage):
            shard = flip(row_me, t << (bit + 1))
            pos = position(shard * per_row + k, col_me, col_bits)
            i = (g * rows + (1 << stage) - 1 + t) * per_row + k
            block = signed.at[g, :, pos]
            copies.append(remote(block, block, (g_sem.at[0, i], g_sem.at[1, i]), {"row": flip(row_me, 1 << bit)}))
        return copies

    def keep_tiles(j):
        c, s = j // 2, j % 2
        k_copy(j).wait()

        def one(t, carry):
            factor = mask[s, pl.ds(t, 1), pl.ds(pl.multiple_of(c * chunk, chunk), chunk)]
            factor = jnp.broadcast_to(factor, (16, chunk)).astype(BF16)
            at = pl.ds(pl.multiple_of(t * TILE, TILE), TILE)
            block = held[j, at, :].reshape(TILE // 16, 16, chunk)
            held[j, at, :] = (block * factor[None]).reshape(TILE, chunk)
            return carry

        lax.fori_loop(0, cd_width // TILE, one, 0)

    def make_signed(g, k):
        f_copy(g, k).wait()
        pos = position(row_me * per_row + k, col_me, col_bits)
        at = pl.ds(k * own + g * part, part)
        for t in range(cd_width // TILE):
            lanes = pl.ds(t * TILE, TILE)
            index = jnp.broadcast_to(cd_lane[pl.ds(t, 1), :], (part, TILE))
            flipped = jnp.take_along_axis(arrived[at, lanes], index, axis=1)
            mine = direct[at, lanes]
            signed[g, 0, pos, :, lanes] = (mine + flipped).astype(BF16)
            signed[g, 1, pos, :, lanes] = (mine - flipped).astype(BF16)

    for g in range(groups):
        for k in range(per_row):
            f_copy(g, k).start()

    def start_k(j, carry):
        k_copy(j).start()
        return carry

    lax.fori_loop(0, 2 * chunks, start_k, 0)

    for k in range(per_row):
        lo, hi = 2 * chunks * k // per_row, 2 * chunks * (k + 1) // per_row

        def keep_step(j, carry):
            keep_tiles(j)
            return carry

        lax.fori_loop(lo, hi, keep_step, 0)
        make_signed(0, k)
        for copy in gather_copies(0, 0, k):
            copy.start()

    def gather_event(g, stage):
        for k in range(per_row):
            if stage == 0:
                make_signed(g, k)
            else:
                for copy in gather_copies(g, stage - 1, k):
                    copy.wait()
            if stage < row_bits:
                for copy in gather_copies(g, stage, k):
                    copy.start()

    for stage in range(1, row_bits + 1):
        gather_event(0, stage)

    def stage_copy(b, q):
        return remote(sends[b].at[q], recvs[b].at[q], (r_sem.at[0, b, q], r_sem.at[1, b, q]),
                      {"col": flip(col_me, 1 << b)})

    def mirror_copy(q):
        return remote(msend.at[q], mrecv.at[q], (m_sem.at[0, q], m_sem.at[1, q]),
                      {"row": flip(row_me, rows // 2)})

    def multiply(q):
        g, c = q // chunks, q % chunks
        for s in range(2):
            lhs = signed[g, s].reshape(cols * part, cd_width)
            total = jnp.dot(lhs, held[2 * c + s], preferred_element_type=F32)
            half = cols * part // 2
            acc[q, s] = total[:half]
            sends[0][q, s] = total[half:].astype(BF16)
        stage_copy(0, q).start()

    def reduce(b, q):
        stage_copy(b - 1, q).wait()
        half = (cols >> b) * part // 2
        for s in range(2):
            sends[b][q, s] = (acc[q, s, half:2 * half] + recvs[b - 1][q, s, half:2 * half].astype(F32)).astype(BF16)
            acc[q, s, :half] = acc[q, s, :half] + recvs[b - 1][q, s, :half].astype(F32)
        stage_copy(b, q).start()

    def combine(q):
        g, c = q // chunks, q % chunks
        stage_copy(col_bits - 1, q).wait()
        plus = acc[q, 0, :part] + recvs[-1][q, 0].astype(F32)
        minus = acc[q, 1, :part] + recvs[-1][q, 1].astype(F32)
        out0[pl.ds(pl.multiple_of(g * part, part), part), pl.ds(pl.multiple_of(c * chunk, chunk), chunk)] = 0.5 * (plus + minus)
        msend[q] = (0.5 * (plus - minus)).astype(BF16)
        mirror_copy(q).start()

    def place(q):
        g, c = q // chunks, q % chunks
        mirror_copy(q).wait()
        for t in range(chunk // TILE):
            target = jnp.broadcast_to(ab_lane[pl.ds(c * (chunk // TILE) + t, 1), :], (TILE, TILE))
            hit = lax.broadcasted_iota(jnp.int32, (TILE, TILE), 0) == target
            chosen = jnp.where(hit, 1.0, 0.0).astype(BF16)
            moved = lax.dot_general(mrecv[q, :, pl.ds(t * TILE, TILE)], chosen, (((1,), (1,)), ((), ())), preferred_element_type=F32)
            out1[pl.ds(pl.multiple_of(g * part, part), part),
                 pl.ds(pl.multiple_of(c * chunk + t * TILE, TILE), TILE)] = moved

    def step(i, carry):
        for g in range(1, groups):
            for stage in range(row_bits + 1):
                when = g * chunks - (0 if stage == row_bits else row_bits + 1 - stage)

                @pl.when(i == when)
                def _():
                    gather_event(g, stage)

        @pl.when(i < pieces)
        def _():
            multiply(i)

        lag = 0
        for b in range(1, col_bits):
            lag += 2 if b == 1 else 1

            @pl.when((i >= lag) & (i < pieces + lag))
            def _():
                reduce(b, i - lag)

        lag += 1

        @pl.when((i >= lag) & (i < pieces + lag))
        def _():
            combine(i - lag)

        lag += 1

        @pl.when((i >= lag) & (i < pieces + lag))
        def _():
            place(i - lag)

        return carry

    lax.fori_loop(0, pieces + col_bits + 2, step, 0)


def body(amplitudes, integrals, screen, mirror, denominators):
    cols, rows = lax.axis_size("col"), lax.axis_size("row")
    col_bits = cols.bit_length() - 1
    occ, _, cd_width = amplitudes.shape
    own, _, ab_width = denominators.shape
    per_row = occ // own
    groups = 2 if own % 32 == 0 else 1
    part = own // groups
    chunk = min(512, ab_width)
    chunks = ab_width // chunk
    pieces = groups * chunks
    ab_partner = (lax.axis_index("row") + rows // 2) % rows * ab_width
    lanes = mirror % TILE
    cd_lane = lax.dynamic_slice_in_dim(lanes, lax.axis_index("col") * cd_width, cd_width).reshape(-1, TILE)
    ab_lane = lax.dynamic_slice_in_dim(lanes, ab_partner, ab_width).reshape(-1, TILE)
    mask = jnp.repeat(screen.astype(F32), TILE, axis=2)
    vmem = pl.BlockSpec(memory_space=pltpu.VMEM)
    shape = lambda b: (pieces, 2, (cols >> b + 1) * part, chunk)
    out0, out1 = pl.pallas_call(
        functools.partial(kernel, (rows, cols, groups, chunk)),
        out_shape=[jax.ShapeDtypeStruct((own, ab_width), F32)] * 2,
        in_specs=[vmem] * 5 + [pl.BlockSpec(memory_space=pl.ANY)],
        out_specs=[vmem] * 2,
        scratch_shapes=[
            pltpu.VMEM((2 * chunks, cd_width, chunk), BF16),
            pltpu.VMEM((occ, cd_width), F32),
            pltpu.VMEM((groups, 2, cols, part, cd_width), BF16),
            pltpu.VMEM(shape(0), F32),
        ] + [pltpu.VMEM(shape(b), BF16) for b in range(col_bits)] * 2 + [
            pltpu.VMEM((pieces, part, chunk), BF16),
            pltpu.VMEM((pieces, part, chunk), BF16),
            pltpu.SemaphoreType.DMA((2 * chunks,)),
            pltpu.SemaphoreType.DMA((2, groups * per_row)),
            pltpu.SemaphoreType.DMA((2, groups * rows * per_row)),
            pltpu.SemaphoreType.DMA((2, col_bits, pieces)),
            pltpu.SemaphoreType.DMA((2, pieces)),
        ],
        compiler_params=pltpu.CompilerParams(
            collective_id=0, has_side_effects=True, vmem_limit_bytes=60 * 1024 * 1024),
    )(amplitudes[:, 0, :], amplitudes[:, 1, :], cd_lane, ab_lane, mask, integrals)
    return jnp.stack([out0, out1], axis=1) / denominators


def solution(mesh):
    in_specs = (
        P("row", None, "col"),
        P(None, "col", "row"),
        P(None, "col", "row"),
        P(),
        P("col", None, "row"),
    )
    out_specs = P("col", None, "row")
    return jax.shard_map(body, mesh=mesh, in_specs=in_specs, out_specs=out_specs, check_vma=False)
```

```python
import functools

import jax
import jax.numpy as jnp
from jax import lax
from jax.experimental import pallas as pl
from jax.experimental.pallas import tpu as pltpu
from jax.sharding import PartitionSpec as P

TILE = 128
F32, BF16 = jnp.float32, jnp.bfloat16


def flip(x, bits):
    result = x
    place = 0
    while bits >> place:
        if bits >> place & 1:
            result = result + (1 - 2 * (x // (1 << place) % 2)) * (1 << place)
        place += 1
    return result


def position(owner, me, bits):
    total = 0
    for i in range(bits):
        differs = (owner // (1 << i) + me // (1 << i)) % 2
        total = total + differs * (1 << (bits - 1 - i))
    return total


def kernel(sizes, direct, mirrored, mirror, mask, integrals, out0, out1,
           held, arrived, signed, acc, *rest):
    rows, cols, groups, chunk = sizes
    row_bits, col_bits = rows.bit_length() - 1, cols.bit_length() - 1
    sends, recvs = rest[:col_bits], rest[col_bits:2 * col_bits]
    msend, mrecv, k_sem, f_sem, g_sem, r_sem, m_sem = rest[2 * col_bits:]
    occ, cd_width = direct.shape
    ab_width = out0.shape[1]
    own = out0.shape[0]
    part = own // groups
    per_row = occ // own
    chunks = ab_width // chunk
    pieces = groups * chunks
    row_me, col_me = lax.axis_index("row"), lax.axis_index("col")

    barrier = pltpu.get_barrier_semaphore()
    for b in range(col_bits):
        pl.semaphore_signal(barrier, inc=1, device_id={"col": flip(col_me, 1 << b)}, device_id_type=pl.DeviceIdType.MESH)
    for b in range(row_bits):
        pl.semaphore_signal(barrier, inc=1, device_id={"row": flip(row_me, 1 << b)}, device_id_type=pl.DeviceIdType.MESH)
    pl.semaphore_wait(barrier, col_bits + row_bits)

    def remote(src, dst, sem, target):
        return pltpu.make_async_remote_copy(
            src_ref=src, dst_ref=dst, send_sem=sem[0], recv_sem=sem[1],
            device_id=target, device_id_type=pl.DeviceIdType.MESH)

    def f_copy(g, k):
        at = pl.ds(k * own + g * part, part)
        i = g * per_row + k
        return remote(mirrored.at[at, :], arrived.at[at, :], (f_sem.at[0, i], f_sem.at[1, i]),
                      {"col": flip(col_me, cols // 2)})

    def k_copy(j):
        c, s = j // 2, j % 2
        return pltpu.make_async_copy(
            integrals.at[s, :, pl.ds(pl.multiple_of(c * chunk, chunk), chunk)], held.at[j], k_sem.at[j])

    def gather_copies(g, stage, k):
        bit = row_bits - 1 - stage
        copies = []
        for t in range(1 << stage):
            shard = flip(row_me, t << (bit + 1))
            pos = position(shard * per_row + k, col_me, col_bits)
            i = (g * rows + (1 << stage) - 1 + t) * per_row + k
            block = signed.at[g, :, pos]
            copies.append(remote(block, block, (g_sem.at[0, i], g_sem.at[1, i]), {"row": flip(row_me, 1 << bit)}))
        return copies

    def keep_tiles(j):
        c, s = j // 2, j % 2
        k_copy(j).wait()

        def one(t, carry):
            factor = mask[s, pl.ds(t, 1), pl.ds(pl.multiple_of(c * chunk, chunk), chunk)]
            factor = jnp.broadcast_to(factor, (16, chunk)).astype(F32).astype(BF16)
            at = pl.ds(pl.multiple_of(t * TILE, TILE), TILE)
            block = held[j, at, :].reshape(TILE // 16, 16, chunk)
            held[j, at, :] = (block * factor[None]).reshape(TILE, chunk)
            return carry

        lax.fori_loop(0, cd_width // TILE, one, 0)

    def make_signed(g, k):
        f_copy(g, k).wait()
        pos = position(row_me * per_row + k, col_me, col_bits)
        at = pl.ds(k * own + g * part, part)
        for t in range(cd_width // TILE):
            lanes = pl.ds(t * TILE, TILE)
            index = jnp.broadcast_to(mirror[pl.ds(col_me * (cd_width // TILE) + t, 1), :] % TILE, (part, TILE))
            flipped = jnp.take_along_axis(arrived[at, lanes], index, axis=1)
            mine = direct[at, lanes]
            signed[g, 0, pos, :, lanes] = (mine + flipped).astype(BF16)
            signed[g, 1, pos, :, lanes] = (mine - flipped).astype(BF16)

    for g in range(groups):
        for k in range(per_row):
            f_copy(g, k).start()

    def start_k(j, carry):
        k_copy(j).start()
        return carry

    lax.fori_loop(0, 2 * chunks, start_k, 0)

    for k in range(per_row):
        lo, hi = 2 * chunks * k // per_row, 2 * chunks * (k + 1) // per_row

        def keep_step(j, carry):
            keep_tiles(j)
            return carry

        lax.fori_loop(lo, hi, keep_step, 0)
        make_signed(0, k)
        for copy in gather_copies(0, 0, k):
            copy.start()

    def gather_event(g, stage):
        for k in range(per_row):
            if stage == 0:
                make_signed(g, k)
            else:
                for copy in gather_copies(g, stage - 1, k):
                    copy.wait()
            if stage < row_bits:
                for copy in gather_copies(g, stage, k):
                    copy.start()

    for stage in range(1, row_bits + 1):
        gather_event(0, stage)

    def stage_copy(b, q):
        return remote(sends[b].at[q], recvs[b].at[q], (r_sem.at[0, b, q], r_sem.at[1, b, q]),
                      {"col": flip(col_me, 1 << b)})

    def mirror_copy(q):
        return remote(msend.at[q], mrecv.at[q], (m_sem.at[0, q], m_sem.at[1, q]),
                      {"row": flip(row_me, rows // 2)})

    def multiply(q):
        g, c = q // chunks, q % chunks
        for s in range(2):
            lhs = signed[g, s].reshape(cols * part, cd_width)
            total = jnp.dot(lhs, held[2 * c + s], preferred_element_type=F32)
            half = cols * part // 2
            acc[q, s] = total[:half]
            sends[0][q, s] = total[half:].astype(BF16)
        stage_copy(0, q).start()

    def reduce(b, q):
        stage_copy(b - 1, q).wait()
        half = (cols >> b) * part // 2
        for s in range(2):
            sends[b][q, s] = (acc[q, s, half:2 * half] + recvs[b - 1][q, s, half:2 * half].astype(F32)).astype(BF16)
            acc[q, s, :half] = acc[q, s, :half] + recvs[b - 1][q, s, :half].astype(F32)
        stage_copy(b, q).start()

    def combine(q):
        g, c = q // chunks, q % chunks
        stage_copy(col_bits - 1, q).wait()
        plus = acc[q, 0, :part] + recvs[-1][q, 0].astype(F32)
        minus = acc[q, 1, :part] + recvs[-1][q, 1].astype(F32)
        out0[pl.ds(pl.multiple_of(g * part, part), part), pl.ds(pl.multiple_of(c * chunk, chunk), chunk)] = 0.5 * (plus + minus)
        msend[q] = (0.5 * (plus - minus)).astype(BF16)
        mirror_copy(q).start()

    def place(q):
        g, c = q // chunks, q % chunks
        mirror_copy(q).wait()
        for t in range(chunk // TILE):
            at = flip(row_me, rows // 2) * (ab_width // TILE) + c * (chunk // TILE) + t
            target = jnp.broadcast_to(mirror[pl.ds(at, 1), :] % TILE, (TILE, TILE))
            hit = lax.broadcasted_iota(jnp.int32, (TILE, TILE), 0) == target
            chosen = jnp.where(hit, 1.0, 0.0).astype(BF16)
            moved = lax.dot_general(mrecv[q, :, pl.ds(t * TILE, TILE)], chosen, (((1,), (1,)), ((), ())), preferred_element_type=F32)
            out1[pl.ds(pl.multiple_of(g * part, part), part),
                 pl.ds(pl.multiple_of(c * chunk + t * TILE, TILE), TILE)] = moved

    def step(i, carry):
        for g in range(1, groups):
            for stage in range(row_bits + 1):
                when = g * chunks - (0 if stage == row_bits else row_bits + 1 - stage)

                @pl.when(i == when)
                def _():
                    gather_event(g, stage)

        @pl.when(i < pieces)
        def _():
            multiply(i)

        lag = 0
        for b in range(1, col_bits):
            lag += 2 if b == 1 else 1

            @pl.when((i >= lag) & (i < pieces + lag))
            def _():
                reduce(b, i - lag)

        lag += 1

        @pl.when((i >= lag) & (i < pieces + lag))
        def _():
            combine(i - lag)

        lag += 1

        @pl.when((i >= lag) & (i < pieces + lag))
        def _():
            place(i - lag)

        return carry

    lax.fori_loop(0, pieces + col_bits + 2, step, 0)


def body(amplitudes, integrals, screen, mirror, denominators):
    cols, rows = lax.axis_size("col"), lax.axis_size("row")
    col_bits = cols.bit_length() - 1
    occ, _, cd_width = amplitudes.shape
    own, _, ab_width = denominators.shape
    per_row = occ // own
    groups = 2 if own % 32 == 0 else 1
    part = own // groups
    chunk = min(1024, ab_width)
    chunks = ab_width // chunk
    pieces = groups * chunks
    vmem = pl.BlockSpec(memory_space=pltpu.VMEM)
    shape = lambda b: (pieces, 2, (cols >> b + 1) * part, chunk)
    out0, out1 = pl.pallas_call(
        functools.partial(kernel, (rows, cols, groups, chunk)),
        out_shape=[jax.ShapeDtypeStruct((own, ab_width), F32)] * 2,
        in_specs=[vmem] * 4 + [pl.BlockSpec(memory_space=pl.ANY)],
        out_specs=[vmem] * 2,
        scratch_shapes=[
            pltpu.VMEM((2 * chunks, cd_width, chunk), BF16),
            pltpu.VMEM((occ, cd_width), F32),
            pltpu.VMEM((groups, 2, cols, part, cd_width), BF16),
            pltpu.VMEM(shape(0), F32),
        ] + [pltpu.VMEM(shape(b), BF16) for b in range(col_bits)] * 2 + [
            pltpu.VMEM((pieces, part, chunk), BF16),
            pltpu.VMEM((pieces, part, chunk), BF16),
            pltpu.SemaphoreType.DMA((2 * chunks,)),
            pltpu.SemaphoreType.DMA((2, groups * per_row)),
            pltpu.SemaphoreType.DMA((2, groups * rows * per_row)),
            pltpu.SemaphoreType.DMA((2, col_bits, pieces)),
            pltpu.SemaphoreType.DMA((2, pieces)),
        ],
        compiler_params=pltpu.CompilerParams(
            collective_id=0, has_side_effects=True, vmem_limit_bytes=60 * 1024 * 1024),
    )(amplitudes[:, 0, :], amplitudes[:, 1, :], mirror.reshape(-1, TILE), jnp.repeat(screen, TILE, axis=2), integrals)
    return jnp.stack([out0, out1], axis=1) / denominators


def solution(mesh):
    in_specs = (
        P("row", None, "col"),
        P(None, "col", "row"),
        P(None, "col", "row"),
        P(),
        P("col", None, "row"),
    )
    out_specs = P("col", None, "row")
    return jax.shard_map(body, mesh=mesh, in_specs=in_specs, out_specs=out_specs, check_vma=False)
```
